256 devices in a mesh: gr: 16 (over x, z_hi, core), gc: 16 (over y, z_lo).
Axes of the slice: x: 4, y: 4, z: 8 (z_hi: 2, z_lo: 4; z = z_hi * 4 + z_lo), core: 2. Of those that a mesh axis runs over, the one named last changes fastest.
Arguments:
- coords: float32 [64, 8192], P(None, ('gr', 'gc')), may hold values from -6 to 6
- mode_scales: float32 [64], replicated, may hold values from 0.002 to 0.5
- rhs_values: float32 [4, 8192], P(None, ('gr', 'gc')), may hold values from -6 to 6
- rhs_grads: float32 [4096, 256], P(('gr', 'gc')), may hold values from -6 to 6
- grad_local: int32 [4096], P(('gr', 'gc')), may hold values from 0 to 31, as said below
- live_counts: int32 [256], P(('gr', 'gc')), may hold values from 1 to 16, as said below
Outputs:
- solution_values: float32 [4, 8192], P(None, ('gr', 'gc'))
- solution_grads: float32 [4096, 256], P(('gr', 'gc'))
The draws below stay inside these ranges and needn't reach their ends.
Inputs may be any that keep to these rules, and one draw needn't show every extreme that they name: `grad_local`: the 16 slots of one device name different designs among its 32; only the first live_counts of them are live. `live_counts`: some device has 16 live slots.
All inputs are finite; a program needn't handle non-finite values.
Results may differ from the reference program's by a relative error of at most 0.0003.
Values sent between devices are 32-bit elements; how exact they have to be, the bound alone decides.
A program may use at most 64 MiB of HBM per device.

```python
import math
import jax
import jax.numpy as jnp
from jax import lax

D = 64
NV = 4
GROUP = 32
ITERS = 3
CAP = 16
N = 8192
GSLOTS = 4096


def draw_grad_local(key, part):
    device_count = GSLOTS // CAP
    keys = jax.random.split(key, device_count)
    chosen = jax.vmap(lambda one_key: jax.random.permutation(one_key, GROUP)[:CAP])(keys)
    return chosen.reshape(-1).astype(jnp.int32)


def draw_live_counts(key, part):
    device_count = GSLOTS // CAP
    first_key, second_key = jax.random.split(jax.random.fold_in(key, 17))
    uniform_pick = jax.random.randint(first_key, (device_count,), 0, CAP)
    counted = 1 + uniform_pick * uniform_pick // CAP
    busiest = jax.random.randint(second_key, (), 0, device_count)
    counted = counted.at[busiest].set(CAP)
    return counted.astype(jnp.int32)


def level_of(stream_key, dims, cuts, least, high):
    def one(position, blocks):
        heights = jax.random.uniform(jax.random.fold_in(jax.random.fold_in(stream_key, 6), position), (blocks,), jnp.float32, least / len(cuts), high / len(cuts))
        return jnp.repeat(jnp.exp(heights), dims[position] // blocks).reshape((-1,) + (1,) * (len(dims) - position - 1))

    factor_of = one(*cuts[0])
    for cut in cuts[1:]:
        factor_of = factor_of * one(*cut)
    return factor_of


def centred(stream_key, dims, scale, bound, cuts=(), kind=jnp.bfloat16):
    array = scale * jax.random.normal(stream_key, dims, jnp.float32)
    if cuts:
        array = array * level_of(stream_key, dims, cuts, -0.22, 0.18)
    return jnp.clip(array, -bound, bound).astype(kind)


def setup_inputs(seed: int = 0) -> dict:
    key_list = jax.random.split(jax.random.key(seed), 7)
    return {
        "coords": centred(key_list[0], (D, N), 1.0, 6.0, ((1, 256),), jnp.float32),
        "mode_scales": jnp.clip(jnp.exp(jax.random.uniform(key_list[1], (D,), jnp.float32, math.log(0.002), math.log(0.5))), 0.002, 0.5),
        "rhs_values": centred(key_list[2], (NV, N), 1.0, 6.0, ((1, 256),), jnp.float32),
        "rhs_grads": centred(key_list[3], (GSLOTS, D * NV), 1.0, 6.0, ((0, 256),), jnp.float32),
        "grad_local": draw_grad_local(jax.random.fold_in(key_list[6], 71), 0),
        "live_counts": draw_live_counts(jax.random.fold_in(key_list[6], 71), 0),
    }


HIGHEST = lax.Precision.HIGHEST
NUGGET = 0.25


def contract_first(left_arr, right_arr):
    return lax.dot_general(left_arr, right_arr, (((0,), (0,)), ((), ())), precision=HIGHEST, preferred_element_type=jnp.float32)


def kernel_tile(first_pts, second_pts, scales):
    first_norm = jnp.sum(scales[:, None] * first_pts * first_pts, axis=0)
    second_norm = jnp.sum(scales[:, None] * second_pts * second_pts, axis=0)
    cross_term = contract_first(first_pts, scales[:, None] * second_pts)
    return jnp.exp(cross_term - 0.5 * (first_norm[:, None] + second_norm[None, :]))


def tile_product(left_pts, left_grad, right_pts, right_grad, right_vals, right_ders, scales):
    widths, grad_count = right_grad.shape
    vectors = right_vals.shape[0]
    left_count = left_pts.shape[1]
    left_grads = left_grad.shape[1]
    right_count = right_pts.shape[1]
    wide_scale = jnp.repeat(scales, vectors)
    scaled_ders = right_ders * wide_scale[None, :]
    scaled_three = scaled_ders.reshape(grad_count, widths, vectors)
    offsets = jnp.sum(right_grad.T[:, :, None] * scaled_three, axis=1)
    value_tile = kernel_tile(right_pts, left_pts, scales)
    cross_tile = kernel_tile(right_grad, left_pts, scales)
    moments = contract_first(cross_tile, scaled_ders)
    value_out = jnp.dot(right_vals, value_tile, precision=HIGHEST)
    value_out = value_out + jnp.einsum("dp,pdv->vp", left_pts, moments.reshape(left_count, widths, vectors), precision=HIGHEST)
    value_out = value_out - contract_first(offsets, cross_tile)
    slope_tile = kernel_tile(right_pts, left_grad, scales)
    weighted = (right_pts.T[:, :, None] * right_vals.T[:, None, :]).reshape(right_count, widths * vectors)
    first_sum = contract_first(slope_tile, right_vals.T)
    second_sum = contract_first(slope_tile, weighted)
    pair_tile = kernel_tile(right_grad, left_grad, scales)
    direct_sum = contract_first(pair_tile, right_ders)
    projected = jnp.einsum("dp,gdv->vgp", left_grad, scaled_three, precision=HIGHEST) - offsets.T[:, :, None]
    weighted_pairs = pair_tile[None, :, :] * projected
    pair_total = jnp.sum(weighted_pairs, axis=1).T
    pair_moment = jnp.einsum("ag,vgp->pav", right_grad, weighted_pairs, precision=HIGHEST)
    combined = second_sum.reshape(left_grads, widths, vectors) + pair_moment - left_grad.T[:, :, None] * (first_sum + pair_total)[:, None, :]
    grad_out = wide_scale[None, :] * (direct_sum + combined.reshape(left_grads, widths * vectors))
    return value_out, grad_out


def pair_dots(first_pair, second_pair):
    value_part = jnp.sum(first_pair[0] * second_pair[0], axis=1)
    grad_part = jnp.sum((first_pair[1] * second_pair[1]).reshape(-1, D, NV), axis=(0, 1))
    return value_part + grad_part


def scaled(pair_arg, factor):
    return (pair_arg[0] * factor[:, None], pair_arg[1] * jnp.tile(factor, D)[None, :])


def add_pairs(first_pair, second_pair):
    return (first_pair[0] + second_pair[0], first_pair[1] + second_pair[1])


def reference(coords, mode_scales, rhs_values, rhs_grads, grad_local, live_counts):
    slot_ids = jnp.arange(GSLOTS, dtype=jnp.int32)
    owner_dev = slot_ids // CAP
    designs = owner_dev * GROUP + grad_local.astype(jnp.int32)
    grad_pts = jnp.take(coords, designs, axis=1)
    live_mask = (slot_ids % CAP < jnp.take(live_counts, owner_dev)).astype(jnp.float32)
    per_block = 8
    block_count = N // (per_block * GROUP)
    left_blocks = jnp.moveaxis(coords.reshape(D, block_count, per_block * GROUP), 1, 0)
    left_grad_blocks = jnp.moveaxis(grad_pts.reshape(D, block_count, per_block * CAP), 1, 0)

    def operator(values_vec, grads_vec):
        def one_block(pieces):
            return tile_product(pieces[0], pieces[1], coords, grad_pts, values_vec, grads_vec, mode_scales)

        value_parts, grad_parts = lax.map(one_block, (left_blocks, left_grad_blocks))
        value_out = jnp.moveaxis(value_parts, 0, 1).reshape(NV, N)
        grad_out = grad_parts.reshape(GSLOTS, D * NV)
        return (value_out + NUGGET * values_vec, (grad_out + NUGGET * grads_vec) * live_mask[:, None])

    residual = (rhs_values, rhs_grads * live_mask[:, None])
    solution = (jnp.zeros_like(rhs_values), jnp.zeros_like(rhs_grads))
    direction = residual
    norm_now = pair_dots(residual, residual)
    for iteration in range(ITERS):
        product_pair = operator(direction[0], direction[1])
        step_size = norm_now / pair_dots(direction, product_pair)
        solution = add_pairs(solution, scaled(direction, step_size))
        residual = add_pairs(residual, scaled(product_pair, -step_size))
        norm_next = pair_dots(residual, residual)
        direction = add_pairs(residual, scaled(direction, norm_next / norm_now))
        norm_now = norm_next
    return solution[0], solution[1]
```

```python
import jax
import jax.numpy as jnp
from jax import lax
from jax.sharding import PartitionSpec as P

D = 64
NV = 4
ITERS = 3
CAP = 16


HIGHEST = lax.Precision.HIGHEST
NUGGET = 0.25


def contract_first(left_arr, right_arr):
    return lax.dot_general(
        left_arr,
        right_arr,
        (((0,), (0,)), ((), ())),
        precision=HIGHEST,
        preferred_element_type=jnp.float32,
    )


def kernel_tile(first_pts, second_pts, scales):
    first_norm = jnp.sum(scales[:, None] * first_pts * first_pts, axis=0)
    second_norm = jnp.sum(scales[:, None] * second_pts * second_pts, axis=0)
    cross_term = contract_first(first_pts, scales[:, None] * second_pts)
    return jnp.exp(cross_term - 0.5 * (first_norm[:, None] + second_norm[None, :]))


def tile_product(left_pts, left_grad, right_pts, right_grad, right_vals, right_ders, scales):
    widths, grad_count = right_grad.shape
    vectors = right_vals.shape[0]
    left_count = left_pts.shape[1]
    left_grads = left_grad.shape[1]
    right_count = right_pts.shape[1]
    wide_scale = jnp.repeat(scales, vectors)
    scaled_ders = right_ders * wide_scale[None, :]
    scaled_three = scaled_ders.reshape(grad_count, widths, vectors)
    offsets = jnp.sum(right_grad.T[:, :, None] * scaled_three, axis=1)
    value_tile = kernel_tile(right_pts, left_pts, scales)
    cross_tile = kernel_tile(right_grad, left_pts, scales)
    moments = contract_first(cross_tile, scaled_ders)
    value_out = jnp.dot(right_vals, value_tile, precision=HIGHEST)
    value_out = value_out + jnp.einsum(
        "dp,pdv->vp", left_pts, moments.reshape(left_count, widths, vectors), precision=HIGHEST
    )
    value_out = value_out - contract_first(offsets, cross_tile)
    slope_tile = kernel_tile(right_pts, left_grad, scales)
    weighted = (right_pts.T[:, :, None] * right_vals.T[:, None, :]).reshape(
        right_count, widths * vectors
    )
    first_sum = contract_first(slope_tile, right_vals.T)
    second_sum = contract_first(slope_tile, weighted)
    pair_tile = kernel_tile(right_grad, left_grad, scales)
    direct_sum = contract_first(pair_tile, right_ders)
    projected = (
        jnp.einsum("dp,gdv->vgp", left_grad, scaled_three, precision=HIGHEST)
        - offsets.T[:, :, None]
    )
    weighted_pairs = pair_tile[None, :, :] * projected
    pair_total = jnp.sum(weighted_pairs, axis=1).T
    pair_moment = jnp.einsum("ag,vgp->pav", right_grad, weighted_pairs, precision=HIGHEST)
    combined = (
        second_sum.reshape(left_grads, widths, vectors)
        + pair_moment
        - left_grad.T[:, :, None] * (first_sum + pair_total)[:, None, :]
    )
    grad_out = wide_scale[None, :] * (direct_sum + combined.reshape(left_grads, widths * vectors))
    return (value_out, grad_out)


def pair_dots(first_pair, second_pair):
    value_part = jnp.sum(first_pair[0] * second_pair[0], axis=1)
    grad_part = jnp.sum((first_pair[1] * second_pair[1]).reshape(-1, D, NV), axis=(0, 1))
    return value_part + grad_part


def gather_a2a(flat, axis, size):
    wide = jnp.broadcast_to(flat[None], (size,) + flat.shape)
    return lax.all_to_all(wide, axis, 0, 0, tiled=True)


def sum_a2a(pieces, axis):
    return jnp.sum(lax.all_to_all(pieces, axis, 0, 0, tiled=True), axis=0)


def pad_rows(flat, width=128):
    extra = (-flat.shape[-1]) % width
    flat = jnp.pad(flat, [(0, 0)] * (flat.ndim - 1) + [(0, extra)])
    return flat.reshape(flat.shape[:-1] + (flat.shape[-1] // width, width))


def body(coords, mode_scales, rhs_values, rhs_grads, grad_local, live_counts):
    n_gr = lax.psum(1, "gr")
    n_gc = lax.psum(1, "gc")
    group = coords.shape[1]
    cap = grad_local.shape[0]
    width = rhs_grads.shape[1]
    grad_pts = jnp.take(coords, grad_local, axis=1)
    live_mask = (jnp.arange(cap, dtype=jnp.int32) < live_counts[0]).astype(jnp.float32)
    own_pts = jnp.concatenate([coords, grad_pts], axis=1)
    n_pts = own_pts.size

    rows = gather_a2a(own_pts.reshape(-1), "gc", n_gc).reshape(n_gc, D, group + cap)
    row_pts = jnp.moveaxis(rows[:, :, :group], 0, 1).reshape(D, n_gc * group)
    row_grad = jnp.moveaxis(rows[:, :, group:], 0, 1).reshape(D, n_gc * cap)

    own_flat = jnp.concatenate(
        [own_pts.reshape(-1), rhs_values.reshape(-1), rhs_grads.reshape(-1), live_mask]
    )
    cols = gather_a2a(own_flat, "gr", n_gr)
    col_pts3 = cols[:, :n_pts].reshape(n_gr, D, group + cap)
    col_pts = jnp.moveaxis(col_pts3[:, :, :group], 0, 1).reshape(D, n_gr * group)
    col_grad = jnp.moveaxis(col_pts3[:, :, group:], 0, 1).reshape(D, n_gr * cap)
    at = n_pts
    vals_c = cols[:, at:at + NV * group].reshape(n_gr, NV, group)
    vals_c = jnp.moveaxis(vals_c, 0, 1).reshape(NV, n_gr * group)
    at += NV * group
    grads_c = cols[:, at:at + cap * width].reshape(n_gr * cap, width)
    at += cap * width
    mask_c = cols[:, at:at + cap].reshape(n_gr * cap)

    residual = (vals_c, grads_c * mask_c[:, None])
    solution = (jnp.zeros_like(vals_c), jnp.zeros_like(grads_c))
    direction = residual
    norm_now = None
    for iteration in range(ITERS):
        value_sum, grad_sum = tile_product(
            row_pts, row_grad, col_pts, col_grad, direction[0], direction[1], mode_scales
        )
        pieces = jnp.concatenate(
            [
                jnp.moveaxis(value_sum.reshape(NV, n_gc, group), 1, 0).reshape(n_gc, NV * group),
                grad_sum.reshape(n_gc, cap * width),
            ],
            axis=1,
        )
        own_prod = sum_a2a(pad_rows(pieces), "gc").reshape(-1)
        prod = gather_a2a(own_prod, "gr", n_gr)
        prod_vals = jnp.moveaxis(prod[:, :NV * group].reshape(n_gr, NV, group), 0, 1)
        prod_vals = prod_vals.reshape(NV, n_gr * group)
        prod_grads = prod[:, NV * group:NV * group + cap * width].reshape(n_gr * cap, width)
        image = (
            prod_vals + NUGGET * direction[0],
            (prod_grads + NUGGET * direction[1]) * mask_c[:, None],
        )
        parts = [pair_dots(direction, image)]
        if iteration + 1 < ITERS:
            parts += [pair_dots(residual, image), pair_dots(image, image)]
        if iteration == 0:
            parts += [pair_dots(residual, residual)]
        partial = jnp.concatenate(parts)
        total = sum_a2a(
            pad_rows(jnp.broadcast_to(partial[None], (n_gc,) + partial.shape)), "gc"
        ).reshape(-1)
        if iteration == 0:
            norm_now = total[len(parts) * NV - NV:len(parts) * NV]
        step_size = norm_now / total[:NV]
        solution = (
            solution[0] + step_size[:, None] * direction[0],
            solution[1] + jnp.tile(step_size, D)[None, :] * direction[1],
        )
        if iteration + 1 < ITERS:
            residual = (
                residual[0] - step_size[:, None] * image[0],
                residual[1] - jnp.tile(step_size, D)[None, :] * image[1],
            )
            cross = total[NV:2 * NV]
            image_norm = total[2 * NV:3 * NV]
            norm_next = norm_now - 2.0 * step_size * cross + step_size * step_size * image_norm
            ratio = norm_next / norm_now
            direction = (
                residual[0] + ratio[:, None] * direction[0],
                residual[1] + jnp.tile(ratio, D)[None, :] * direction[1],
            )
            norm_now = norm_next
    me = lax.axis_index("gr")
    out_vals = lax.dynamic_slice_in_dim(solution[0], me * group, group, axis=1)
    out_grads = lax.dynamic_slice_in_dim(solution[1], me * cap, cap, axis=0)
    return (out_vals, out_grads)


def solution(mesh):
    in_specs = (
        P(None, ("gr", "gc")),
        P(),
        P(None, ("gr", "gc")),
        P(("gr", "gc"), None),
        P(("gr", "gc")),
        P(("gr", "gc")),
    )
    out_specs = (P(None, ("gr", "gc")), P(("gr", "gc"), None))
    return jax.shard_map(body, mesh=mesh, in_specs=in_specs, out_specs=out_specs, check_vma=False)
```

```python
import jax
import jax.numpy as jnp
from jax import lax
from jax.sharding import PartitionSpec as P

D = 64
NV = 4
ITERS = 3
CAP = 16


HIGHEST = lax.Precision.HIGHEST
NUGGET = 0.25


def contract_first(left_arr, right_arr):
    return lax.dot_general(
        left_arr,
        right_arr,
        (((0,), (0,)), ((), ())),
        precision=HIGHEST,
        preferred_element_type=jnp.float32,
    )


def kernel_tile(first_pts, second_pts, scales):
    first_norm = jnp.sum(scales[:, None] * first_pts * first_pts, axis=0)
    second_norm = jnp.sum(scales[:, None] * second_pts * second_pts, axis=0)
    cross_term = contract_first(first_pts, scales[:, None] * second_pts)
    return jnp.exp(cross_term - 0.5 * (first_norm[:, None] + second_norm[None, :]))


def tile_product(left_pts, left_grad, right_pts, right_grad, right_vals, right_ders, scales):
    widths, grad_count = right_grad.shape
    vectors = right_vals.shape[0]
    left_count = left_pts.shape[1]
    left_grads = left_grad.shape[1]
    right_count = right_pts.shape[1]
    wide_scale = lax.optimization_barrier(jnp.repeat(scales, vectors))
    scaled_ders = right_ders * wide_scale[None, :]
    scaled_three = scaled_ders.reshape(grad_count, widths, vectors)
    offsets = jnp.sum(right_grad.T[:, :, None] * scaled_three, axis=1)
    value_tile = kernel_tile(right_pts, left_pts, scales)
    cross_tile = kernel_tile(right_grad, left_pts, scales)
    moments = contract_first(cross_tile, scaled_ders)
    value_out = jnp.dot(right_vals, value_tile, precision=HIGHEST)
    value_out = value_out + jnp.einsum(
        "dp,pdv->vp", left_pts, moments.reshape(left_count, widths, vectors), precision=HIGHEST
    )
    value_out = value_out - contract_first(offsets, cross_tile)
    slope_tile = kernel_tile(right_pts, left_grad, scales)
    weighted = (right_pts.T[:, :, None] * right_vals.T[:, None, :]).reshape(
        right_count, widths * vectors
    )
    first_sum = contract_first(slope_tile, right_vals.T)
    second_sum = contract_first(slope_tile, weighted)
    pair_tile = kernel_tile(right_grad, left_grad, scales)
    direct_sum = contract_first(pair_tile, right_ders)
    projected = (
        jnp.einsum("dp,gdv->vgp", left_grad, scaled_three, precision=HIGHEST)
        - offsets.T[:, :, None]
    )
    weighted_pairs = pair_tile[None, :, :] * projected
    pair_total = jnp.sum(weighted_pairs, axis=1).T
    pair_moment = jnp.einsum("ag,vgp->pav", right_grad, weighted_pairs, precision=HIGHEST)
    combined = (
        second_sum.reshape(left_grads, widths, vectors)
        + pair_moment
        - left_grad.T[:, :, None] * (first_sum + pair_total)[:, None, :]
    )
    grad_out = wide_scale[None, :] * (direct_sum + combined.reshape(left_grads, widths * vectors))
    return (value_out, grad_out)


def pair_dots(first_pair, second_pair):
    value_part = jnp.sum(first_pair[0] * second_pair[0], axis=1)
    grad_part = jnp.sum(jnp.sum(first_pair[1] * second_pair[1], axis=0).reshape(D, NV), axis=0)
    return value_part + grad_part


def wide(factor):
    return lax.optimization_barrier(jnp.tile(factor, D))


def gather_a2a(flat, axis, size):
    wide = jnp.broadcast_to(flat[None], (size,) + flat.shape)
    return lax.all_to_all(wide, axis, 0, 0, tiled=True)


def sum_a2a(pieces, axis):
    return jnp.sum(lax.all_to_all(pieces, axis, 0, 0, tiled=True), axis=0)


def pad_rows(flat, width=128):
    extra = (-flat.shape[-1]) % width
    flat = jnp.pad(flat, [(0, 0)] * (flat.ndim - 1) + [(0, extra)])
    return flat.reshape(flat.shape[:-1] + (flat.shape[-1] // width, width))


def body(coords, mode_scales, rhs_values, rhs_grads, grad_local, live_counts):
    n_gr = lax.psum(1, "gr")
    n_gc = lax.psum(1, "gc")
    group = coords.shape[1]
    cap = grad_local.shape[0]
    width = rhs_grads.shape[1]
    grad_pts = jnp.take(coords, grad_local, axis=1)
    live_mask = (jnp.arange(cap, dtype=jnp.int32) < live_counts[0]).astype(jnp.float32)
    own_pts = jnp.concatenate([coords, grad_pts], axis=1)
    n_pts = own_pts.size

    rows = gather_a2a(own_pts.reshape(-1), "gc", n_gc).reshape(n_gc, D, group + cap)
    row_pts = jnp.moveaxis(rows[:, :, :group], 0, 1).reshape(D, n_gc * group)
    row_grad = jnp.moveaxis(rows[:, :, group:], 0, 1).reshape(D, n_gc * cap)

    own_flat = jnp.concatenate(
        [own_pts.reshape(-1), rhs_values.reshape(-1), rhs_grads.reshape(-1), live_mask]
    )
    cols = gather_a2a(own_flat, "gr", n_gr)
    col_pts3 = cols[:, :n_pts].reshape(n_gr, D, group + cap)
    col_pts = jnp.moveaxis(col_pts3[:, :, :group], 0, 1).reshape(D, n_gr * group)
    col_grad = jnp.moveaxis(col_pts3[:, :, group:], 0, 1).reshape(D, n_gr * cap)
    at = n_pts
    vals_c = cols[:, at:at + NV * group].reshape(n_gr, NV, group)
    vals_c = jnp.moveaxis(vals_c, 0, 1).reshape(NV, n_gr * group)
    at += NV * group
    grads_c = cols[:, at:at + cap * width].reshape(n_gr * cap, width)
    at += cap * width
    mask_c = cols[:, at:at + cap].reshape(n_gr * cap)

    residual = (vals_c, grads_c * mask_c[:, None])
    solution = (jnp.zeros_like(vals_c), jnp.zeros_like(grads_c))
    direction = residual
    norm_now = None
    for iteration in range(ITERS):
        value_sum, grad_sum = tile_product(
            row_pts, row_grad, col_pts, col_grad, direction[0], direction[1], mode_scales
        )
        value_rows = jnp.moveaxis(value_sum.reshape(NV, n_gc, group), 1, 0).reshape(n_gc, 1, NV * group)
        pieces = jnp.concatenate(
            [
                grad_sum.reshape(n_gc, cap, width),
                jnp.pad(value_rows, ((0, 0), (0, 0), (0, width - NV * group))),
            ],
            axis=1,
        )
        own_prod = sum_a2a(pieces, "gc")
        prod = gather_a2a(own_prod, "gr", n_gr)
        prod_vals = jnp.moveaxis(prod[:, cap, :NV * group].reshape(n_gr, NV, group), 0, 1)
        prod_vals = prod_vals.reshape(NV, n_gr * group)
        prod_grads = prod[:, :cap, :].reshape(n_gr * cap, width)
        image = (
            prod_vals + NUGGET * direction[0],
            (prod_grads + NUGGET * direction[1]) * mask_c[:, None],
        )
        parts = [pair_dots(direction, image)]
        if iteration + 1 < ITERS:
            parts += [pair_dots(residual, image), pair_dots(image, image)]
        if iteration == 0:
            parts += [pair_dots(residual, residual)]
        partial = jnp.concatenate(parts)
        total = sum_a2a(
            pad_rows(jnp.broadcast_to(partial[None], (n_gc,) + partial.shape)), "gc"
        ).reshape(-1)
        if iteration == 0:
            norm_now = total[len(parts) * NV - NV:len(parts) * NV]
        step_size = norm_now / total[:NV]
        solution = (
            solution[0] + step_size[:, None] * direction[0],
            solution[1] + wide(step_size)[None, :] * direction[1],
        )
        if iteration + 1 < ITERS:
            residual = (
                residual[0] - step_size[:, None] * image[0],
                residual[1] - wide(step_size)[None, :] * image[1],
            )
            cross = total[NV:2 * NV]
            image_norm = total[2 * NV:3 * NV]
            norm_next = norm_now - 2.0 * step_size * cross + step_size * step_size * image_norm
            ratio = norm_next / norm_now
            direction = (
                residual[0] + ratio[:, None] * direction[0],
                residual[1] + wide(ratio)[None, :] * direction[1],
            )
            norm_now = norm_next
    me = lax.axis_index("gr")
    out_vals = lax.dynamic_slice_in_dim(solution[0], me * group, group, axis=1)
    out_grads = lax.dynamic_slice_in_dim(solution[1], me * cap, cap, axis=0)
    return (out_vals, out_grads)


def solution(mesh):
    in_specs = (
        P(None, ("gr", "gc")),
        P(),
        P(None, ("gr", "gc")),
        P(("gr", "gc"), None),
        P(("gr", "gc")),
        P(("gr", "gc")),
    )
    out_specs = (P(None, ("gr", "gc")), P(("gr", "gc"), None))
    return jax.shard_map(body, mesh=mesh, in_specs=in_specs, out_specs=out_specs, check_vma=False)
```

```python
import jax
import jax.numpy as jnp
from jax import lax
from jax.sharding import PartitionSpec as P

D = 64
NV = 4
ITERS = 3
CAP = 16


HIGHEST = lax.Precision.HIGHEST
NUGGET = 0.25


def contract_first(left_arr, right_arr):
    return lax.dot_general(
        left_arr,
        right_arr,
        (((0,), (0,)), ((), ())),
        precision=HIGHEST,
        preferred_element_type=jnp.float32,
    )


def kernel_tile(first_pts, second_pts, scales):
    first_norm = jnp.sum(scales[:, None] * first_pts * first_pts, axis=0)
    second_norm = jnp.sum(scales[:, None] * second_pts * second_pts, axis=0)
    cross_term = contract_first(first_pts, scales[:, None] * second_pts)
    return jnp.exp(cross_term - 0.5 * (first_norm[:, None] + second_norm[None, :]))


def selectors(widths, vectors):
    flat = jnp.arange(widths * vectors, dtype=jnp.int32)
    pick = (flat[:, None] % vectors == jnp.arange(vectors, dtype=jnp.int32)[None, :]).astype(jnp.float32)
    return lax.optimization_barrier(pick)


def spread(matrix, vectors):
    return lax.optimization_barrier(jnp.repeat(matrix, vectors, axis=1))


def mm(left_arr, right_arr):
    return jnp.dot(left_arr, right_arr, precision=HIGHEST, preferred_element_type=jnp.float32)


def prepare(left_pts, left_grad, right_pts, right_grad, scales, vectors):
    widths = right_grad.shape[0]
    pick = selectors(widths, vectors)
    eye = jnp.eye(vectors, dtype=jnp.float32)
    block = (left_grad[:, None, None, :] * eye[None, :, :, None]).reshape(widths * vectors, -1)
    flat = jnp.arange(widths * vectors, dtype=jnp.int32)
    perm = (
        (flat[:, None] % widths) * vectors + flat[:, None] // widths == flat[None, :]
    ).astype(jnp.float32)
    return dict(
        pick=pick,
        block=lax.optimization_barrier(block),
        perm=lax.optimization_barrier(perm),
        wide_scale=lax.optimization_barrier(jnp.repeat(scales, vectors)),
        right_grad_rep=spread(right_grad.T, vectors),
        left_pts_rep=spread(left_pts.T, vectors),
        right_pts_rep=spread(right_pts.T, vectors),
        left_grad_rep=spread(left_grad.T, vectors),
        value_tile=kernel_tile(right_pts, left_pts, scales),
        cross_tile=kernel_tile(right_grad, left_pts, scales),
        slope_tile=kernel_tile(right_pts, left_grad, scales),
        pair_tile=kernel_tile(right_grad, left_grad, scales),
    )


def tile_product(pre, right_grad, right_vals, right_ders):
    widths, grad_count = right_grad.shape
    vectors = right_vals.shape[0]
    left_grads = pre["pair_tile"].shape[1]
    pick = pre["pick"]
    scaled_ders = right_ders * pre["wide_scale"][None, :]
    offsets = mm(scaled_ders * pre["right_grad_rep"], pick)
    cross_tile = pre["cross_tile"]
    moments = contract_first(cross_tile, scaled_ders)
    value_out = mm(right_vals, pre["value_tile"])
    value_out = value_out + mm(moments * pre["left_pts_rep"], pick).T
    value_out = value_out - contract_first(offsets, cross_tile)
    slope_tile = pre["slope_tile"]
    weighted = pre["right_pts_rep"] * mm(right_vals.T, pick.T)
    first_sum = contract_first(slope_tile, right_vals.T)
    second_sum = contract_first(slope_tile, weighted)
    pair_tile = pre["pair_tile"]
    direct_sum = contract_first(pair_tile, right_ders)
    projected = mm(scaled_ders, pre["block"]).reshape(grad_count, vectors, left_grads)
    projected = projected - offsets[:, :, None]
    weighted_pairs = pair_tile[:, None, :] * projected
    pair_total = jnp.sum(weighted_pairs, axis=0).T
    by_v = lax.dot_general(
        weighted_pairs,
        right_grad,
        (((0,), (1,)), ((), ())),
        precision=HIGHEST,
        preferred_element_type=jnp.float32,
    )
    pair_moment = mm(jnp.moveaxis(by_v, 1, 0).reshape(left_grads, vectors * widths), pre["perm"])
    combined = second_sum + pair_moment - pre["left_grad_rep"] * mm(first_sum + pair_total, pick.T)
    grad_out = pre["wide_scale"][None, :] * (direct_sum + combined)
    return (value_out, grad_out)


def pair_dots(first_pair, second_pair):
    value_part = jnp.sum(first_pair[0] * second_pair[0], axis=1)
    grad_part = jnp.sum(jnp.sum(first_pair[1] * second_pair[1], axis=0).reshape(D, NV), axis=0)
    return value_part + grad_part


def wide(factor):
    return lax.optimization_barrier(jnp.tile(factor, D))


def gather_a2a(flat, axis, size):
    wide = jnp.broadcast_to(flat[None], (size,) + flat.shape)
    return lax.all_to_all(wide, axis, 0, 0, tiled=True)


def sum_a2a(pieces, axis):
    return jnp.sum(lax.all_to_all(pieces, axis, 0, 0, tiled=True), axis=0)


def pad_rows(flat, width=128):
    extra = (-flat.shape[-1]) % width
    flat = jnp.pad(flat, [(0, 0)] * (flat.ndim - 1) + [(0, extra)])
    return flat.reshape(flat.shape[:-1] + (flat.shape[-1] // width, width))


def body(coords, mode_scales, rhs_values, rhs_grads, grad_local, live_counts):
    n_gr = lax.psum(1, "gr")
    n_gc = lax.psum(1, "gc")
    group = coords.shape[1]
    cap = grad_local.shape[0]
    width = rhs_grads.shape[1]
    grad_pts = jnp.take(coords, grad_local, axis=1)
    live_mask = (jnp.arange(cap, dtype=jnp.int32) < live_counts[0]).astype(jnp.float32)
    own_pts = jnp.concatenate([coords, grad_pts], axis=1)
    n_pts = own_pts.size

    rows = gather_a2a(own_pts.reshape(-1), "gc", n_gc).reshape(n_gc, D, group + cap)
    row_pts = jnp.moveaxis(rows[:, :, :group], 0, 1).reshape(D, n_gc * group)
    row_grad = jnp.moveaxis(rows[:, :, group:], 0, 1).reshape(D, n_gc * cap)

    own_flat = jnp.concatenate(
        [own_pts.reshape(-1), rhs_values.reshape(-1), rhs_grads.reshape(-1), live_mask]
    )
    cols = gather_a2a(own_flat, "gr", n_gr)
    col_pts3 = cols[:, :n_pts].reshape(n_gr, D, group + cap)
    col_pts = jnp.moveaxis(col_pts3[:, :, :group], 0, 1).reshape(D, n_gr * group)
    col_grad = jnp.moveaxis(col_pts3[:, :, group:], 0, 1).reshape(D, n_gr * cap)
    at = n_pts
    vals_c = cols[:, at:at + NV * group].reshape(n_gr, NV, group)
    vals_c = jnp.moveaxis(vals_c, 0, 1).reshape(NV, n_gr * group)
    at += NV * group
    grads_c = cols[:, at:at + cap * width].reshape(n_gr * cap, width)
    at += cap * width
    mask_c = cols[:, at:at + cap].reshape(n_gr * cap)

    pre = prepare(row_pts, row_grad, col_pts, col_grad, mode_scales, NV)
    residual = (vals_c, grads_c * mask_c[:, None])
    solution = (jnp.zeros_like(vals_c), jnp.zeros_like(grads_c))
    direction = residual
    norm_now = None
    for iteration in range(ITERS):
        value_sum, grad_sum = tile_product(pre, col_grad, direction[0], direction[1])
        value_rows = jnp.moveaxis(value_sum.reshape(NV, n_gc, group), 1, 0).reshape(n_gc, 1, NV * group)
        pieces = jnp.concatenate(
            [
                grad_sum.reshape(n_gc, cap, width),
                jnp.pad(value_rows, ((0, 0), (0, 0), (0, width - NV * group))),
            ],
            axis=1,
        )
        own_prod = sum_a2a(pieces, "gc")
        prod = gather_a2a(own_prod, "gr", n_gr)
        prod_vals = jnp.moveaxis(prod[:, cap, :NV * group].reshape(n_gr, NV, group), 0, 1)
        prod_vals = prod_vals.reshape(NV, n_gr * group)
        prod_grads = prod[:, :cap, :].reshape(n_gr * cap, width)
        image = (
            prod_vals + NUGGET * direction[0],
            (prod_grads + NUGGET * direction[1]) * mask_c[:, None],
        )
        parts = [pair_dots(direction, image)]
        if iteration + 1 < ITERS:
            parts += [pair_dots(residual, image), pair_dots(image, image)]
        if iteration == 0:
            parts += [pair_dots(residual, residual)]
        partial = jnp.concatenate(parts)
        total = sum_a2a(
            pad_rows(jnp.broadcast_to(partial[None], (n_gc,) + partial.shape)), "gc"
        ).reshape(-1)
        if iteration == 0:
            norm_now = total[len(parts) * NV - NV:len(parts) * NV]
        step_size = norm_now / total[:NV]
        solution = (
            solution[0] + step_size[:, None] * direction[0],
            solution[1] + wide(step_size)[None, :] * direction[1],
        )
        if iteration + 1 < ITERS:
            residual = (
                residual[0] - step_size[:, None] * image[0],
                residual[1] - wide(step_size)[None, :] * image[1],
            )
            cross = total[NV:2 * NV]
            image_norm = total[2 * NV:3 * NV]
            norm_next = norm_now - 2.0 * step_size * cross + step_size * step_size * image_norm
            ratio = norm_next / norm_now
            direction = (
                residual[0] + ratio[:, None] * direction[0],
                residual[1] + wide(ratio)[None, :] * direction[1],
            )
            norm_now = norm_next
    me = lax.axis_index("gr")
    out_vals = lax.dynamic_slice_in_dim(solution[0], me * group, group, axis=1)
    out_grads = lax.dynamic_slice_in_dim(solution[1], me * cap, cap, axis=0)
    return (out_vals, out_grads)


def solution(mesh):
    in_specs = (
        P(None, ("gr", "gc")),
        P(),
        P(None, ("gr", "gc")),
        P(("gr", "gc"), None),
        P(("gr", "gc")),
        P(("gr", "gc")),
    )
    out_specs = (P(None, ("gr", "gc")), P(("gr", "gc"), None))
    return jax.shard_map(body, mesh=mesh, in_specs=in_specs, out_specs=out_specs, check_vma=False)
```

```python
import jax
import jax.numpy as jnp
from jax import lax
from jax.sharding import PartitionSpec as P

D = 64
NV = 4
ITERS = 3
CAP = 16


HIGHEST = lax.Precision.HIGHEST
NUGGET = 0.25


def contract_first(left_arr, right_arr):
    return lax.dot_general(
        left_arr,
        right_arr,
        (((0,), (0,)), ((), ())),
        precision=HIGHEST,
        preferred_element_type=jnp.float32,
    )


def kernel_tile(first_pts, second_pts, scales):
    first_norm = jnp.sum(scales[:, None] * first_pts * first_pts, axis=0)
    second_norm = jnp.sum(scales[:, None] * second_pts * second_pts, axis=0)
    cross_term = contract_first(first_pts, scales[:, None] * second_pts)
    return jnp.exp(cross_term - 0.5 * (first_norm[:, None] + second_norm[None, :]))


def selectors(widths, vectors):
    flat = jnp.arange(widths * vectors, dtype=jnp.int32)
    pick = (flat[:, None] % vectors == jnp.arange(vectors, dtype=jnp.int32)[None, :]).astype(jnp.float32)
    return lax.optimization_barrier(pick)


def spread(matrix, vectors):
    return lax.optimization_barrier(jnp.repeat(matrix, vectors, axis=1))


def mm(left_arr, right_arr):
    return jnp.dot(left_arr, right_arr, precision=HIGHEST, preferred_element_type=jnp.float32)


def prepare(left_pts, left_grad, right_pts, right_grad, scales, vectors):
    widths = right_grad.shape[0]
    pick = selectors(widths, vectors)
    eye = jnp.eye(vectors, dtype=jnp.float32)
    block = (left_grad[:, None, None, :] * eye[None, :, :, None]).reshape(widths * vectors, -1)
    flat = jnp.arange(widths * vectors, dtype=jnp.int32)
    perm = (
        (flat[:, None] % widths) * vectors + flat[:, None] // widths == flat[None, :]
    ).astype(jnp.float32)
    return dict(
        pick=pick,
        block=lax.optimization_barrier(block),
        perm=lax.optimization_barrier(perm),
        wide_scale=lax.optimization_barrier(jnp.repeat(scales, vectors)),
        right_grad_rep=spread(right_grad.T, vectors),
        left_pts_rep=spread(left_pts.T, vectors),
        right_pts_rep=spread(right_pts.T, vectors),
        left_grad_rep=spread(left_grad.T, vectors),
        value_tile=kernel_tile(right_pts, left_pts, scales),
        cross_tile=kernel_tile(right_grad, left_pts, scales),
        slope_tile=kernel_tile(right_pts, left_grad, scales),
        pair_tile=kernel_tile(right_grad, left_grad, scales),
    )


def tile_product(pre, right_grad, right_vals, right_ders):
    widths, grad_count = right_grad.shape
    vectors = right_vals.shape[0]
    left_grads = pre["pair_tile"].shape[1]
    pick = pre["pick"]
    scaled_ders = right_ders * pre["wide_scale"][None, :]
    offsets = mm(scaled_ders * pre["right_grad_rep"], pick)
    cross_tile = pre["cross_tile"]
    moments = contract_first(cross_tile, scaled_ders)
    value_out = mm(right_vals, pre["value_tile"])
    value_out = value_out + mm(moments * pre["left_pts_rep"], pick).T
    value_out = value_out - contract_first(offsets, cross_tile)
    slope_tile = pre["slope_tile"]
    weighted = pre["right_pts_rep"] * mm(right_vals.T, pick.T)
    first_sum = contract_first(slope_tile, right_vals.T)
    second_sum = contract_first(slope_tile, weighted)
    pair_tile = pre["pair_tile"]
    direct_sum = contract_first(pair_tile, right_ders)
    projected = mm(scaled_ders, pre["block"]).reshape(grad_count, vectors, left_grads)
    projected = projected - offsets[:, :, None]
    weighted_pairs = pair_tile[:, None, :] * projected
    pair_total = jnp.sum(weighted_pairs, axis=0).T
    by_v = lax.dot_general(
        weighted_pairs,
        right_grad,
        (((0,), (1,)), ((), ())),
        precision=HIGHEST,
        preferred_element_type=jnp.float32,
    )
    pair_moment = mm(jnp.moveaxis(by_v, 1, 0).reshape(left_grads, vectors * widths), pre["perm"])
    combined = second_sum + pair_moment - pre["left_grad_rep"] * mm(first_sum + pair_total, pick.T)
    grad_out = pre["wide_scale"][None, :] * (direct_sum + combined)
    return (value_out, grad_out)


def pair_dots(first_pair, second_pair):
    value_part = jnp.sum(first_pair[0] * second_pair[0], axis=1)
    grad_part = jnp.sum(jnp.sum(first_pair[1] * second_pair[1], axis=0).reshape(D, NV), axis=0)
    return value_part + grad_part


def wide(factor):
    return lax.optimization_barrier(jnp.tile(factor, D))


def gather_a2a(flat, axis, size):
    wide = jnp.broadcast_to(flat[None], (size,) + flat.shape)
    return lax.all_to_all(wide, axis, 0, 0, tiled=True)


def sum_a2a(pieces, axis):
    return jnp.sum(lax.all_to_all(pieces, axis, 0, 0, tiled=True), axis=0)


def pad_rows(flat, width=128):
    extra = (-flat.shape[-1]) % width
    flat = jnp.pad(flat, [(0, 0)] * (flat.ndim - 1) + [(0, extra)])
    return flat.reshape(flat.shape[:-1] + (flat.shape[-1] // width, width))


def body(coords, mode_scales, rhs_values, rhs_grads, grad_local, live_counts):
    n_gr = lax.psum(1, "gr")
    n_gc = lax.psum(1, "gc")
    group = coords.shape[1]
    cap = grad_local.shape[0]
    width = rhs_grads.shape[1]
    grad_pts = jnp.take(coords, grad_local, axis=1)
    live_mask = (jnp.arange(cap, dtype=jnp.int32) < live_counts[0]).astype(jnp.float32)
    own_pts = jnp.concatenate([coords, grad_pts], axis=1)
    n_pts = own_pts.size

    rows = gather_a2a(own_pts.reshape(-1), "gc", n_gc).reshape(n_gc, D, group + cap)
    row_pts = jnp.moveaxis(rows[:, :, :group], 0, 1).reshape(D, n_gc * group)
    row_grad = jnp.moveaxis(rows[:, :, group:], 0, 1).reshape(D, n_gc * cap)

    own_flat = jnp.concatenate(
        [own_pts.reshape(-1), rhs_values.reshape(-1), rhs_grads.reshape(-1), live_mask]
    )
    cols = gather_a2a(own_flat, "gr", n_gr)
    col_pts3 = cols[:, :n_pts].reshape(n_gr, D, group + cap)
    col_pts = jnp.moveaxis(col_pts3[:, :, :group], 0, 1).reshape(D, n_gr * group)
    col_grad = jnp.moveaxis(col_pts3[:, :, group:], 0, 1).reshape(D, n_gr * cap)
    at = n_pts
    vals_c = cols[:, at:at + NV * group].reshape(n_gr, NV, group)
    vals_c = jnp.moveaxis(vals_c, 0, 1).reshape(NV, n_gr * group)
    at += NV * group
    grads_c = cols[:, at:at + cap * width].reshape(n_gr * cap, width)
    at += cap * width
    mask_c = cols[:, at:at + cap].reshape(n_gr * cap)

    pre = prepare(row_pts, row_grad, col_pts, col_grad, mode_scales, NV)
    pick = pre["pick"]
    residual = (vals_c, grads_c * mask_c[:, None])
    solution = (jnp.zeros_like(vals_c), jnp.zeros_like(grads_c))
    direction = residual
    norm_now = None
    for iteration in range(ITERS):
        value_sum, grad_sum = tile_product(pre, col_grad, direction[0], direction[1])
        value_rows = jnp.moveaxis(value_sum.reshape(NV, n_gc, group), 1, 0).reshape(n_gc, 1, NV * group)
        pieces = jnp.concatenate(
            [
                grad_sum.reshape(n_gc, cap, width),
                jnp.pad(value_rows, ((0, 0), (0, 0), (0, width - NV * group))),
            ],
            axis=1,
        )
        own_prod = sum_a2a(pieces, "gc")
        prod = gather_a2a(own_prod, "gr", n_gr)
        prod_vals = jnp.moveaxis(prod[:, cap, :NV * group].reshape(n_gr, NV, group), 0, 1)
        prod_vals = prod_vals.reshape(NV, n_gr * group)
        prod_grads = prod[:, :cap, :].reshape(n_gr * cap, width)
        image = (
            prod_vals + NUGGET * direction[0],
            (prod_grads + NUGGET * direction[1]) * mask_c[:, None],
        )
        pairs = [(direction, image)]
        if iteration + 1 < ITERS:
            pairs += [(residual, image), (image, image)]
        if iteration == 0:
            pairs += [(residual, residual)]
        value_part = jnp.sum(jnp.stack([a[0] * b[0] for a, b in pairs]), axis=2)
        grad_cols = jnp.sum(jnp.stack([a[1] * b[1] for a, b in pairs]), axis=1)
        partial = (value_part + mm(grad_cols, pick)).reshape(-1)
        n_parts = len(pairs)
        partial = jnp.pad(partial, (0, 128 - partial.shape[0]))
        total = sum_a2a(jnp.broadcast_to(partial[None, None], (n_gc, 1, 128)), "gc").reshape(-1)
        if iteration == 0:
            norm_now = total[n_parts * NV - NV:n_parts * NV]
        step_size = norm_now / total[:NV]
        solution = (
            solution[0] + step_size[:, None] * direction[0],
            solution[1] + wide(step_size)[None, :] * direction[1],
        )
        if iteration + 1 < ITERS:
            residual = (
                residual[0] - step_size[:, None] * image[0],
                residual[1] - wide(step_size)[None, :] * image[1],
            )
            cross = total[NV:2 * NV]
            image_norm = total[2 * NV:3 * NV]
            norm_next = norm_now - 2.0 * step_size * cross + step_size * step_size * image_norm
            ratio = norm_next / norm_now
            direction = (
                residual[0] + ratio[:, None] * direction[0],
                residual[1] + wide(ratio)[None, :] * direction[1],
            )
            norm_now = norm_next
    me = lax.axis_index("gr")
    out_vals = lax.dynamic_slice_in_dim(solution[0], me * group, group, axis=1)
    out_grads = lax.dynamic_slice_in_dim(solution[1], me * cap, cap, axis=0)
    return (out_vals, out_grads)


def solution(mesh):
    in_specs = (
        P(None, ("gr", "gc")),
        P(),
        P(None, ("gr", "gc")),
        P(("gr", "gc"), None),
        P(("gr", "gc")),
        P(("gr", "gc")),
    )
    out_specs = (P(None, ("gr", "gc")), P(("gr", "gc"), None))
    return jax.shard_map(body, mesh=mesh, in_specs=in_specs, out_specs=out_specs, check_vma=False)
```

```python
import jax
import jax.numpy as jnp
from jax import lax
from jax.sharding import PartitionSpec as P

D = 64
NV = 4
ITERS = 3
CAP = 16


HIGHEST = lax.Precision.HIGHEST
NUGGET = 0.25


def contract_first(left_arr, right_arr):
    return lax.dot_general(
        left_arr,
        right_arr,
        (((0,), (0,)), ((), ())),
        precision=HIGHEST,
        preferred_element_type=jnp.float32,
    )


def kernel_tile(first_pts, second_pts, scales):
    first_norm = jnp.sum(scales[:, None] * first_pts * first_pts, axis=0)
    second_norm = jnp.sum(scales[:, None] * second_pts * second_pts, axis=0)
    cross_term = contract_first(first_pts, scales[:, None] * second_pts)
    return jnp.exp(cross_term - 0.5 * (first_norm[:, None] + second_norm[None, :]))


def selectors(widths, vectors):
    flat = jnp.arange(widths * vectors, dtype=jnp.int32)
    pick = (flat[:, None] % vectors == jnp.arange(vectors, dtype=jnp.int32)[None, :]).astype(jnp.float32)
    return lax.optimization_barrier(pick)


def spread(matrix, vectors):
    widths = matrix.shape[1]
    flat = jnp.arange(widths * vectors, dtype=jnp.int32)
    copy_of = (flat[None, :] // vectors == jnp.arange(widths, dtype=jnp.int32)[:, None]).astype(jnp.float32)
    return mm(matrix, lax.optimization_barrier(copy_of))


def mm(left_arr, right_arr):
    return jnp.dot(left_arr, right_arr, precision=HIGHEST, preferred_element_type=jnp.float32)


def prepare(left_pts, left_grad, right_pts, right_grad, scales, vectors):
    widths = right_grad.shape[0]
    pick = selectors(widths, vectors)
    eye = jnp.eye(vectors, dtype=jnp.float32)
    block = (left_grad[:, None, None, :] * eye[None, :, :, None]).reshape(widths * vectors, -1)
    flat = jnp.arange(widths * vectors, dtype=jnp.int32)
    perm = (
        (flat[:, None] % widths) * vectors + flat[:, None] // widths == flat[None, :]
    ).astype(jnp.float32)
    return dict(
        pick=pick,
        block=lax.optimization_barrier(block),
        perm=lax.optimization_barrier(perm),
        wide_scale=lax.optimization_barrier(jnp.repeat(scales, vectors)),
        right_grad_rep=spread(right_grad.T, vectors),
        left_pts_rep=spread(left_pts.T, vectors),
        right_pts_rep=spread(right_pts.T, vectors),
        left_grad_rep=spread(left_grad.T, vectors),
        value_tile=kernel_tile(right_pts, left_pts, scales),
        cross_tile=kernel_tile(right_grad, left_pts, scales),
        slope_tile=kernel_tile(right_pts, left_grad, scales),
        pair_tile=kernel_tile(right_grad, left_grad, scales),
    )


def tile_product(pre, right_grad, right_vals, right_ders):
    widths, grad_count = right_grad.shape
    vectors = right_vals.shape[0]
    left_grads = pre["pair_tile"].shape[1]
    pick = pre["pick"]
    scaled_ders = right_ders * pre["wide_scale"][None, :]
    offsets = mm(scaled_ders * pre["right_grad_rep"], pick)
    cross_tile = pre["cross_tile"]
    moments = contract_first(cross_tile, scaled_ders)
    value_out = mm(right_vals, pre["value_tile"])
    value_out = value_out + mm(moments * pre["left_pts_rep"], pick).T
    value_out = value_out - contract_first(offsets, cross_tile)
    slope_tile = pre["slope_tile"]
    weighted = pre["right_pts_rep"] * mm(right_vals.T, pick.T)
    first_sum = contract_first(slope_tile, right_vals.T)
    second_sum = contract_first(slope_tile, weighted)
    pair_tile = pre["pair_tile"]
    direct_sum = contract_first(pair_tile, right_ders)
    projected = mm(scaled_ders, pre["block"]).reshape(grad_count, vectors, left_grads)
    projected = projected - offsets[:, :, None]
    weighted_pairs = pair_tile[:, None, :] * projected
    pair_total = jnp.sum(weighted_pairs, axis=0).T
    by_v = lax.dot_general(
        weighted_pairs,
        right_grad,
        (((0,), (1,)), ((), ())),
        precision=HIGHEST,
        preferred_element_type=jnp.float32,
    )
    pair_moment = mm(jnp.moveaxis(by_v, 1, 0).reshape(left_grads, vectors * widths), pre["perm"])
    combined = second_sum + pair_moment - pre["left_grad_rep"] * mm(first_sum + pair_total, pick.T)
    grad_out = pre["wide_scale"][None, :] * (direct_sum + combined)
    return (value_out, grad_out)


def pair_dots(first_pair, second_pair):
    value_part = jnp.sum(first_pair[0] * second_pair[0], axis=1)
    grad_part = jnp.sum(jnp.sum(first_pair[1] * second_pair[1], axis=0).reshape(D, NV), axis=0)
    return value_part + grad_part


def wide(factor):
    return lax.optimization_barrier(jnp.tile(factor, D))


def gather_a2a(flat, axis, size):
    wide = jnp.broadcast_to(flat[None], (size,) + flat.shape)
    return lax.all_to_all(wide, axis, 0, 0, tiled=True)


def sum_a2a(pieces, axis):
    return jnp.sum(lax.all_to_all(pieces, axis, 0, 0, tiled=True), axis=0)


def pad_rows(flat, width=128):
    extra = (-flat.shape[-1]) % width
    flat = jnp.pad(flat, [(0, 0)] * (flat.ndim - 1) + [(0, extra)])
    return flat.reshape(flat.shape[:-1] + (flat.shape[-1] // width, width))


def body(coords, mode_scales, rhs_values, rhs_grads, grad_local, live_counts):
    n_gr = lax.psum(1, "gr")
    n_gc = lax.psum(1, "gc")
    group = coords.shape[1]
    cap = grad_local.shape[0]
    width = rhs_grads.shape[1]
    grad_pts = jnp.take(coords, grad_local, axis=1)
    live_mask = (jnp.arange(cap, dtype=jnp.int32) < live_counts[0]).astype(jnp.float32)
    own_pts = jnp.concatenate([coords, grad_pts], axis=1)
    n_pts = own_pts.size

    rows = gather_a2a(own_pts.reshape(-1), "gc", n_gc).reshape(n_gc, D, group + cap)
    row_pts = jnp.moveaxis(rows[:, :, :group], 0, 1).reshape(D, n_gc * group)
    row_grad = jnp.moveaxis(rows[:, :, group:], 0, 1).reshape(D, n_gc * cap)

    own_flat = jnp.concatenate(
        [own_pts.reshape(-1), rhs_values.reshape(-1), rhs_grads.reshape(-1), live_mask]
    )
    cols = gather_a2a(own_flat, "gr", n_gr)
    col_pts3 = cols[:, :n_pts].reshape(n_gr, D, group + cap)
    col_pts = jnp.moveaxis(col_pts3[:, :, :group], 0, 1).reshape(D, n_gr * group)
    col_grad = jnp.moveaxis(col_pts3[:, :, group:], 0, 1).reshape(D, n_gr * cap)
    at = n_pts
    vals_c = cols[:, at:at + NV * group].reshape(n_gr, NV, group)
    vals_c = jnp.moveaxis(vals_c, 0, 1).reshape(NV, n_gr * group)
    at += NV * group
    grads_c = cols[:, at:at + cap * width].reshape(n_gr * cap, width)
    at += cap * width
    mask_c = cols[:, at:at + cap].reshape(n_gr * cap)

    pre = prepare(row_pts, row_grad, col_pts, col_grad, mode_scales, NV)
    pick = pre["pick"]
    residual = (vals_c, grads_c * mask_c[:, None])
    solution = (jnp.zeros_like(vals_c), jnp.zeros_like(grads_c))
    direction = residual
    norm_now = None
    for iteration in range(ITERS):
        value_sum, grad_sum = tile_product(pre, col_grad, direction[0], direction[1])
        value_rows = jnp.moveaxis(value_sum.reshape(NV, n_gc, group), 1, 0).reshape(n_gc, 1, NV * group)
        pieces = jnp.concatenate(
            [
                grad_sum.reshape(n_gc, cap, width),
                jnp.pad(value_rows, ((0, 0), (0, 0), (0, width - NV * group))),
            ],
            axis=1,
        )
        own_prod = sum_a2a(pieces, "gc")
        prod = gather_a2a(own_prod, "gr", n_gr)
        prod_vals = jnp.moveaxis(prod[:, cap, :NV * group].reshape(n_gr, NV, group), 0, 1)
        prod_vals = prod_vals.reshape(NV, n_gr * group)
        prod_grads = prod[:, :cap, :].reshape(n_gr * cap, width)
        image = (
            prod_vals + NUGGET * direction[0],
            (prod_grads + NUGGET * direction[1]) * mask_c[:, None],
        )
        pairs = [(direction, image)]
        if iteration + 1 < ITERS:
            pairs += [(residual, image), (image, image)]
        if iteration == 0:
            pairs += [(residual, residual)]
        value_part = jnp.sum(jnp.stack([a[0] * b[0] for a, b in pairs]), axis=2)
        grad_cols = jnp.sum(jnp.stack([a[1] * b[1] for a, b in pairs]), axis=1)
        partial = (value_part + mm(grad_cols, pick)).reshape(-1)
        n_parts = len(pairs)
        partial = jnp.pad(partial, (0, 128 - partial.shape[0]))
        total = sum_a2a(jnp.broadcast_to(partial[None, None], (n_gc, 1, 128)), "gc").reshape(-1)
        if iteration == 0:
            norm_now = total[n_parts * NV - NV:n_parts * NV]
        step_size = norm_now / total[:NV]
        solution = (
            solution[0] + step_size[:, None] * direction[0],
            solution[1] + wide(step_size)[None, :] * direction[1],
        )
        if iteration + 1 < ITERS:
            residual = (
                residual[0] - step_size[:, None] * image[0],
                residual[1] - wide(step_size)[None, :] * image[1],
            )
            cross = total[NV:2 * NV]
            image_norm = total[2 * NV:3 * NV]
            norm_next = norm_now - 2.0 * step_size * cross + step_size * step_size * image_norm
            ratio = norm_next / norm_now
            direction = (
                residual[0] + ratio[:, None] * direction[0],
                residual[1] + wide(ratio)[None, :] * direction[1],
            )
            norm_now = norm_next
    me = lax.axis_index("gr")
    out_vals = lax.dynamic_slice_in_dim(solution[0], me * group, group, axis=1)
    out_grads = lax.dynamic_slice_in_dim(solution[1], me * cap, cap, axis=0)
    return (out_vals, out_grads)


def solution(mesh):
    in_specs = (
        P(None, ("gr", "gc")),
        P(),
        P(None, ("gr", "gc")),
        P(("gr", "gc"), None),
        P(("gr", "gc")),
        P(("gr", "gc")),
    )
    out_specs = (P(None, ("gr", "gc")), P(("gr", "gc"), None))
    return jax.shard_map(body, mesh=mesh, in_specs=in_specs, out_specs=out_specs, check_vma=False)
```

```python
import jax
import jax.numpy as jnp
from jax import lax
from jax.sharding import PartitionSpec as P

D = 64
NV = 4
ITERS = 3
CAP = 16


HIGHEST = lax.Precision.HIGHEST
NUGGET = 0.25


def contract_first(left_arr, right_arr):
    return lax.dot_general(
        left_arr,
        right_arr,
        (((0,), (0,)), ((), ())),
        precision=HIGHEST,
        preferred_element_type=jnp.float32,
    )


def kernel_tile(first_pts, second_pts, scales):
    first_norm = jnp.sum(scales[:, None] * first_pts * first_pts, axis=0)
    second_norm = jnp.sum(scales[:, None] * second_pts * second_pts, axis=0)
    cross_term = contract_first(first_pts, scales[:, None] * second_pts)
    return jnp.exp(cross_term - 0.5 * (first_norm[:, None] + second_norm[None, :]))


def selectors(widths, vectors):
    flat = jnp.arange(widths * vectors, dtype=jnp.int32)
    pick = (flat[:, None] % vectors == jnp.arange(vectors, dtype=jnp.int32)[None, :]).astype(jnp.float32)
    return lax.optimization_barrier(pick)


def spread(matrix, vectors):
    widths = matrix.shape[1]
    flat = jnp.arange(widths * vectors, dtype=jnp.int32)
    copy_of = (flat[None, :] // vectors == jnp.arange(widths, dtype=jnp.int32)[:, None]).astype(jnp.float32)
    return mm(matrix, lax.optimization_barrier(copy_of))


def mm(left_arr, right_arr):
    return jnp.dot(left_arr, right_arr, precision=HIGHEST, preferred_element_type=jnp.float32)


def prepare(left_pts, left_grad, right_pts, right_grad, scales, vectors):
    widths = right_grad.shape[0]
    pick = selectors(widths, vectors)
    eye = jnp.eye(vectors, dtype=jnp.float32)
    block = (left_grad[:, None, None, :] * eye[None, :, :, None]).reshape(widths * vectors, -1)
    flat = jnp.arange(widths * vectors, dtype=jnp.int32)
    perm = (
        (flat[:, None] % widths) * vectors + flat[:, None] // widths == flat[None, :]
    ).astype(jnp.float32)
    return dict(
        pick=pick,
        block=lax.optimization_barrier(block),
        perm=lax.optimization_barrier(perm),
        wide_scale=lax.optimization_barrier(jnp.repeat(scales, vectors)),
        right_grad_rep=spread(right_grad.T, vectors),
        left_pts_rep=spread(left_pts.T, vectors),
        right_pts_rep=spread(right_pts.T, vectors),
        left_grad_rep=spread(left_grad.T, vectors),
        value_tile=kernel_tile(right_pts, left_pts, scales),
        cross_tile=kernel_tile(right_grad, left_pts, scales),
        slope_tile=kernel_tile(right_pts, left_grad, scales),
        pair_tile=kernel_tile(right_grad, left_grad, scales),
    )


def tile_product(pre, right_grad, right_vals, right_ders):
    widths, grad_count = right_grad.shape
    vectors = right_vals.shape[0]
    left_grads = pre["pair_tile"].shape[1]
    pick = pre["pick"]
    scaled_ders = right_ders * pre["wide_scale"][None, :]
    offsets = mm(scaled_ders * pre["right_grad_rep"], pick)
    cross_tile = pre["cross_tile"]
    moments = contract_first(cross_tile, scaled_ders)
    value_out = mm(right_vals, pre["value_tile"])
    value_out = value_out + contract_first(pick, (moments * pre["left_pts_rep"]).T)
    value_out = value_out - contract_first(offsets, cross_tile)
    slope_tile = pre["slope_tile"]
    weighted = pre["right_pts_rep"] * mm(right_vals.T, pick.T)
    first_sum = mm(right_vals, slope_tile)
    second_sum = contract_first(slope_tile, weighted)
    pair_tile = pre["pair_tile"]
    direct_sum = contract_first(pair_tile, right_ders)
    projected = mm(scaled_ders, pre["block"]).reshape(grad_count, vectors, left_grads)
    projected = projected - offsets[:, :, None]
    weighted_pairs = pair_tile[:, None, :] * projected
    pair_total = jnp.sum(weighted_pairs, axis=0)
    by_v = lax.dot_general(
        weighted_pairs,
        right_grad,
        (((0,), (1,)), ((), ())),
        precision=HIGHEST,
        preferred_element_type=jnp.float32,
    )
    pair_moment = mm(jnp.moveaxis(by_v, 1, 0).reshape(left_grads, vectors * widths), pre["perm"])
    combined = second_sum + pair_moment - pre["left_grad_rep"] * contract_first(first_sum + pair_total, pick.T)
    grad_out = pre["wide_scale"][None, :] * (direct_sum + combined)
    return (value_out, grad_out)


def pair_dots(first_pair, second_pair):
    value_part = jnp.sum(first_pair[0] * second_pair[0], axis=1)
    grad_part = jnp.sum(jnp.sum(first_pair[1] * second_pair[1], axis=0).reshape(D, NV), axis=0)
    return value_part + grad_part


def wide(factor):
    return lax.optimization_barrier(jnp.tile(factor, D))


def gather_a2a(flat, axis, size):
    wide = jnp.broadcast_to(flat[None], (size,) + flat.shape)
    return lax.all_to_all(wide, axis, 0, 0, tiled=True)


def sum_a2a(pieces, axis):
    return jnp.sum(lax.all_to_all(pieces, axis, 0, 0, tiled=True), axis=0)


def pad_rows(flat, width=128):
    extra = (-flat.shape[-1]) % width
    flat = jnp.pad(flat, [(0, 0)] * (flat.ndim - 1) + [(0, extra)])
    return flat.reshape(flat.shape[:-1] + (flat.shape[-1] // width, width))


def body(coords, mode_scales, rhs_values, rhs_grads, grad_local, live_counts):
    n_gr = lax.psum(1, "gr")
    n_gc = lax.psum(1, "gc")
    group = coords.shape[1]
    cap = grad_local.shape[0]
    width = rhs_grads.shape[1]
    grad_pts = jnp.take(coords, grad_local, axis=1)
    live_mask = (jnp.arange(cap, dtype=jnp.int32) < live_counts[0]).astype(jnp.float32)
    own_pts = jnp.concatenate([coords, grad_pts], axis=1)
    n_pts = own_pts.size

    rows = gather_a2a(own_pts.reshape(-1), "gc", n_gc).reshape(n_gc, D, group + cap)
    row_pts = jnp.moveaxis(rows[:, :, :group], 0, 1).reshape(D, n_gc * group)
    row_grad = jnp.moveaxis(rows[:, :, group:], 0, 1).reshape(D, n_gc * cap)

    own_flat = jnp.concatenate(
        [own_pts.reshape(-1), rhs_values.reshape(-1), rhs_grads.reshape(-1), live_mask]
    )
    cols = gather_a2a(own_flat, "gr", n_gr)
    col_pts3 = cols[:, :n_pts].reshape(n_gr, D, group + cap)
    col_pts = jnp.moveaxis(col_pts3[:, :, :group], 0, 1).reshape(D, n_gr * group)
    col_grad = jnp.moveaxis(col_pts3[:, :, group:], 0, 1).reshape(D, n_gr * cap)
    at = n_pts
    vals_c = cols[:, at:at + NV * group].reshape(n_gr, NV, group)
    vals_c = jnp.moveaxis(vals_c, 0, 1).reshape(NV, n_gr * group)
    at += NV * group
    grads_c = cols[:, at:at + cap * width].reshape(n_gr * cap, width)
    at += cap * width
    mask_c = cols[:, at:at + cap].reshape(n_gr * cap)

    pre = prepare(row_pts, row_grad, col_pts, col_grad, mode_scales, NV)
    pick = pre["pick"]
    residual = (vals_c, grads_c * mask_c[:, None])
    solution = (jnp.zeros_like(vals_c), jnp.zeros_like(grads_c))
    direction = residual
    norm_now = None
    for iteration in range(ITERS):
        value_sum, grad_sum = tile_product(pre, col_grad, direction[0], direction[1])
        value_rows = jnp.moveaxis(value_sum.reshape(NV, n_gc, group), 1, 0).reshape(n_gc, 1, NV * group)
        pieces = jnp.concatenate(
            [
                grad_sum.reshape(n_gc, cap, width),
                jnp.pad(value_rows, ((0, 0), (0, 0), (0, width - NV * group))),
            ],
            axis=1,
        )
        own_prod = sum_a2a(pieces, "gc")
        prod = gather_a2a(own_prod, "gr", n_gr)
        prod_vals = jnp.moveaxis(prod[:, cap, :NV * group].reshape(n_gr, NV, group), 0, 1)
        prod_vals = prod_vals.reshape(NV, n_gr * group)
        prod_grads = prod[:, :cap, :].reshape(n_gr * cap, width)
        image = (
            prod_vals + NUGGET * direction[0],
            (prod_grads + NUGGET * direction[1]) * mask_c[:, None],
        )
        pairs = [(direction, image)]
        if iteration + 1 < ITERS:
            pairs += [(residual, image), (image, image)]
        if iteration == 0:
            pairs += [(residual, residual)]
        value_part = jnp.sum(jnp.stack([a[0] * b[0] for a, b in pairs]), axis=2)
        grad_cols = jnp.sum(jnp.stack([a[1] * b[1] for a, b in pairs]), axis=1)
        partial = (value_part + mm(grad_cols, pick)).reshape(-1)
        n_parts = len(pairs)
        partial = jnp.pad(partial, (0, 128 - partial.shape[0]))
        total = sum_a2a(jnp.broadcast_to(partial[None, None], (n_gc, 1, 128)), "gc").reshape(-1)
        if iteration == 0:
            norm_now = total[n_parts * NV - NV:n_parts * NV]
        step_size = norm_now / total[:NV]
        solution = (
            solution[0] + step_size[:, None] * direction[0],
            solution[1] + wide(step_size)[None, :] * direction[1],
        )
        if iteration + 1 < ITERS:
            residual = (
                residual[0] - step_size[:, None] * image[0],
                residual[1] - wide(step_size)[None, :] * image[1],
            )
            cross = total[NV:2 * NV]
            image_norm = total[2 * NV:3 * NV]
            norm_next = norm_now - 2.0 * step_size * cross + step_size * step_size * image_norm
            ratio = norm_next / norm_now
            direction = (
                residual[0] + ratio[:, None] * direction[0],
                residual[1] + wide(ratio)[None, :] * direction[1],
            )
            norm_now = norm_next
    me = lax.axis_index("gr")
    out_vals = lax.dynamic_slice_in_dim(solution[0], me * group, group, axis=1)
    out_grads = lax.dynamic_slice_in_dim(solution[1], me * cap, cap, axis=0)
    return (out_vals, out_grads)


def solution(mesh):
    in_specs = (
        P(None, ("gr", "gc")),
        P(),
        P(None, ("gr", "gc")),
        P(("gr", "gc"), None),
        P(("gr", "gc")),
        P(("gr", "gc")),
    )
    out_specs = (P(None, ("gr", "gc")), P(("gr", "gc"), None))
    return jax.shard_map(body, mesh=mesh, in_specs=in_specs, out_specs=out_specs, check_vma=False)
```

```python
import jax
import jax.numpy as jnp
from jax import lax
from jax.sharding import PartitionSpec as P

D = 64
NV = 4
ITERS = 3
CAP = 16


HIGHEST = lax.Precision.HIGHEST
NUGGET = 0.25


def contract_first(left_arr, right_arr):
    return lax.dot_general(
        left_arr,
        right_arr,
        (((0,), (0,)), ((), ())),
        precision=HIGHEST,
        preferred_element_type=jnp.float32,
    )


def kernel_tile(first_pts, second_pts, scales):
    first_norm = jnp.sum(scales[:, None] * first_pts * first_pts, axis=0)
    second_norm = jnp.sum(scales[:, None] * second_pts * second_pts, axis=0)
    cross_term = contract_first(first_pts, scales[:, None] * second_pts)
    return jnp.exp(cross_term - 0.5 * (first_norm[:, None] + second_norm[None, :]))


def selectors(widths, vectors):
    flat = jnp.arange(widths * vectors, dtype=jnp.int32)
    pick = (flat[:, None] % vectors == jnp.arange(vectors, dtype=jnp.int32)[None, :]).astype(jnp.float32)
    return lax.optimization_barrier(pick)


def spread(matrix, vectors):
    widths = matrix.shape[1]
    flat = jnp.arange(widths * vectors, dtype=jnp.int32)
    copy_of = (flat[None, :] // vectors == jnp.arange(widths, dtype=jnp.int32)[:, None]).astype(jnp.float32)
    return mm(matrix, lax.optimization_barrier(copy_of))


def mm(left_arr, right_arr):
    return jnp.dot(left_arr, right_arr, precision=HIGHEST, preferred_element_type=jnp.float32)


def prepare(left_pts, left_grad, right_pts, right_grad, scales, vectors):
    widths = right_grad.shape[0]
    pick = selectors(widths, vectors)
    eye = jnp.eye(vectors, dtype=jnp.float32)
    block = (left_grad[:, None, None, :] * eye[None, :, :, None]).reshape(widths * vectors, -1)
    flat = jnp.arange(widths * vectors, dtype=jnp.int32)
    perm = (
        (flat[:, None] % widths) * vectors + flat[:, None] // widths == flat[None, :]
    ).astype(jnp.float32)
    return dict(
        pick=pick,
        block=lax.optimization_barrier(block),
        perm=lax.optimization_barrier(perm),
        wide_scale=lax.optimization_barrier(jnp.repeat(scales, vectors)),
        right_grad_rep=spread(right_grad.T, vectors),
        left_pts_rep=spread(left_pts.T, vectors),
        right_pts_rep=spread(right_pts.T, vectors),
        left_grad_rep=spread(left_grad.T, vectors),
        value_tile=kernel_tile(right_pts, left_pts, scales),
        cross_tile=kernel_tile(right_grad, left_pts, scales),
        slope_tile=kernel_tile(right_pts, left_grad, scales),
        pair_tile=kernel_tile(right_grad, left_grad, scales),
    )


def tile_product(pre, right_grad, right_vals, right_ders):
    widths, grad_count = right_grad.shape
    vectors = right_vals.shape[0]
    left_grads = pre["pair_tile"].shape[1]
    pick = pre["pick"]
    scaled_ders = right_ders * pre["wide_scale"][None, :]
    offsets = mm(scaled_ders * pre["right_grad_rep"], pick)
    cross_tile = pre["cross_tile"]
    moments = contract_first(cross_tile, scaled_ders)
    value_out = mm(right_vals, pre["value_tile"])
    value_out = value_out + contract_first(pick, (moments * pre["left_pts_rep"]).T)
    value_out = value_out - contract_first(offsets, cross_tile)
    slope_tile = pre["slope_tile"]
    weighted = pre["right_pts_rep"] * mm(right_vals.T, pick.T)
    first_sum = mm(right_vals, slope_tile)
    second_sum = contract_first(slope_tile, weighted)
    pair_tile = pre["pair_tile"]
    direct_sum = contract_first(pair_tile, right_ders)
    projected = mm(scaled_ders, pre["block"]).reshape(grad_count, vectors, left_grads)
    projected = projected - offsets[:, :, None]
    weighted_pairs = pair_tile[:, None, :] * projected
    pair_total = jnp.sum(weighted_pairs, axis=0)
    by_v = lax.dot_general(
        weighted_pairs,
        right_grad,
        (((0,), (1,)), ((), ())),
        precision=HIGHEST,
        preferred_element_type=jnp.float32,
    )
    pair_moment = mm(jnp.moveaxis(by_v, 1, 0).reshape(left_grads, vectors * widths), pre["perm"])
    combined = second_sum + pair_moment - pre["left_grad_rep"] * contract_first(first_sum + pair_total, pick.T)
    grad_out = pre["wide_scale"][None, :] * (direct_sum + combined)
    return (value_out, grad_out)


def pair_dots(first_pair, second_pair):
    value_part = jnp.sum(first_pair[0] * second_pair[0], axis=1)
    grad_part = jnp.sum(jnp.sum(first_pair[1] * second_pair[1], axis=0).reshape(D, NV), axis=0)
    return value_part + grad_part


def wide(factor):
    return lax.optimization_barrier(jnp.tile(factor, D))


def gather_a2a(flat, axis, size):
    wide = jnp.broadcast_to(flat[None], (size,) + flat.shape)
    return lax.all_to_all(wide, axis, 0, 0, tiled=True)


def sum_a2a(pieces, axis):
    return jnp.sum(lax.all_to_all(pieces, axis, 0, 0, tiled=True), axis=0)


def pad_rows(flat, width=128):
    extra = (-flat.shape[-1]) % width
    flat = jnp.pad(flat, [(0, 0)] * (flat.ndim - 1) + [(0, extra)])
    return flat.reshape(flat.shape[:-1] + (flat.shape[-1] // width, width))


def body(coords, mode_scales, rhs_values, rhs_grads, grad_local, live_counts):
    n_gr = lax.psum(1, "gr")
    n_gc = lax.psum(1, "gc")
    group = coords.shape[1]
    cap = grad_local.shape[0]
    width = rhs_grads.shape[1]
    grad_pts = jnp.take(coords, grad_local, axis=1)
    live_mask = (jnp.arange(cap, dtype=jnp.int32) < live_counts[0]).astype(jnp.float32)
    own_pts = jnp.concatenate([coords, grad_pts], axis=1)
    n_pts = own_pts.size

    rows = gather_a2a(own_pts.reshape(-1), "gc", n_gc).reshape(n_gc, D, group + cap)
    row_pts = jnp.moveaxis(rows[:, :, :group], 0, 1).reshape(D, n_gc * group)
    row_grad = jnp.moveaxis(rows[:, :, group:], 0, 1).reshape(D, n_gc * cap)

    own_flat = jnp.concatenate(
        [own_pts.reshape(-1), rhs_values.reshape(-1), rhs_grads.reshape(-1), live_mask]
    )
    cols = gather_a2a(own_flat, "gr", n_gr)
    col_pts3 = cols[:, :n_pts].reshape(n_gr, D, group + cap)
    col_pts = jnp.moveaxis(col_pts3[:, :, :group], 0, 1).reshape(D, n_gr * group)
    col_grad = jnp.moveaxis(col_pts3[:, :, group:], 0, 1).reshape(D, n_gr * cap)
    at = n_pts
    vals_c = cols[:, at:at + NV * group].reshape(n_gr, NV, group)
    vals_c = jnp.moveaxis(vals_c, 0, 1).reshape(NV, n_gr * group)
    at += NV * group
    grads_c = cols[:, at:at + cap * width].reshape(n_gr * cap, width)
    at += cap * width
    mask_c = cols[:, at:at + cap].reshape(n_gr * cap)

    pre = prepare(row_pts, row_grad, col_pts, col_grad, mode_scales, NV)
    pick = pre["pick"]
    residual = (vals_c, grads_c * mask_c[:, None])
    solution = (jnp.zeros_like(vals_c), jnp.zeros_like(grads_c))
    direction = residual

    def one_iteration(iteration, state):
        solution, residual, direction = state
        value_sum, grad_sum = tile_product(pre, col_grad, direction[0], direction[1])
        value_rows = jnp.moveaxis(value_sum.reshape(NV, n_gc, group), 1, 0).reshape(n_gc, 1, NV * group)
        pieces = jnp.concatenate(
            [
                grad_sum.reshape(n_gc, cap, width),
                jnp.pad(value_rows, ((0, 0), (0, 0), (0, width - NV * group))),
            ],
            axis=1,
        )
        own_prod = sum_a2a(pieces, "gc")
        prod = gather_a2a(own_prod, "gr", n_gr)
        prod_vals = jnp.moveaxis(prod[:, cap, :NV * group].reshape(n_gr, NV, group), 0, 1)
        prod_vals = prod_vals.reshape(NV, n_gr * group)
        prod_grads = prod[:, :cap, :].reshape(n_gr * cap, width)
        image = (
            prod_vals + NUGGET * direction[0],
            (prod_grads + NUGGET * direction[1]) * mask_c[:, None],
        )
        pairs = [(direction, image), (residual, image), (image, image), (residual, residual)]
        value_part = jnp.sum(jnp.stack([a[0] * b[0] for a, b in pairs]), axis=2)
        grad_cols = jnp.sum(jnp.stack([a[1] * b[1] for a, b in pairs]), axis=1)
        partial = (value_part + mm(grad_cols, pick)).reshape(-1)
        partial = jnp.pad(partial, (0, 128 - partial.shape[0]))
        total = sum_a2a(jnp.broadcast_to(partial[None, None], (n_gc, 1, 128)), "gc").reshape(-1)
        norm_now = total[3 * NV:4 * NV]
        step_size = norm_now / total[:NV]
        solution = (
            solution[0] + step_size[:, None] * direction[0],
            solution[1] + wide(step_size)[None, :] * direction[1],
        )
        residual = (
            residual[0] - step_size[:, None] * image[0],
            residual[1] - wide(step_size)[None, :] * image[1],
        )
        cross = total[NV:2 * NV]
        image_norm = total[2 * NV:3 * NV]
        norm_next = norm_now - 2.0 * step_size * cross + step_size * step_size * image_norm
        ratio = norm_next / norm_now
        direction = (
            residual[0] + ratio[:, None] * direction[0],
            residual[1] + wide(ratio)[None, :] * direction[1],
        )
        return (solution, residual, direction)

    solution, residual, direction = lax.fori_loop(
        0, ITERS, one_iteration, (solution, residual, direction)
    )
    me = lax.axis_index("gr")
    out_vals = lax.dynamic_slice_in_dim(solution[0], me * group, group, axis=1)
    out_grads = lax.dynamic_slice_in_dim(solution[1], me * cap, cap, axis=0)
    return (out_vals, out_grads)


def solution(mesh):
    in_specs = (
        P(None, ("gr", "gc")),
        P(),
        P(None, ("gr", "gc")),
        P(("gr", "gc"), None),
        P(("gr", "gc")),
        P(("gr", "gc")),
    )
    out_specs = (P(None, ("gr", "gc")), P(("gr", "gc"), None))
    return jax.shard_map(body, mesh=mesh, in_specs=in_specs, out_specs=out_specs, check_vma=False)
```
